32 devices in a mesh: grp: 2 (over y), seq: 4 (over z), mdl: 2 (over x), sub: 2 (over core).
Axes of the slice: x: 2, y: 2, z: 4, core: 2. Of those that a mesh axis runs over, the one named last changes fastest.
Arguments:
- frames: bfloat16 [2048, 1280], P(('grp', 'seq', 'mdl')), parts along dimension 0, may hold values from -6 to 6
- audio_count: int32 [16], P(('grp', 'seq', 'mdl')), parts along dimension 0, may hold values from 1 to 127
- pos_ids: int32 [3, 2048], P(None, ('grp', 'seq', 'mdl')), parts along dimension 1, may hold values from 0 to 4095
- gain_audio: float32 [1280], replicated, may hold values from 0.1 to 1.9
- gain_video: float32 [1280], replicated, may hold values from 0.1 to 1.9
- audio_proj: bfloat16 [1280, 3584], P(('seq', 'mdl'), 'sub'), may hold values from -0.15625 to 0.15625
- video_proj: bfloat16 [1280, 3584], P(('seq', 'mdl'), 'sub'), may hold values from -0.15625 to 0.15625
- dest_device: int32 [2048], P(('grp', 'seq', 'mdl')), parts along dimension 0, may hold values from 0 to 7, as said below
- dest_slot: int32 [2048], P(('grp', 'seq', 'mdl')), parts along dimension 0, may hold values from 0 to 127, as said below
Outputs:
- lm_rows: bfloat16 [2048, 3584], P(('grp', 'seq', 'mdl'), 'sub'), parts along dimension 0
The draws below stay inside these ranges and needn't reach their ends.
There are 2 independent parts, one for each index of `grp`. The reference program is written for one: setup_inputs(seed, part) draws one part's arguments, and reference() takes and returns one part's arrays. A program takes and returns all parts, laid end to end along the dimension named above; an argument that names none is the same for every part. Nothing has to cross between parts.
Inputs may be any that keep to these rules, and one draw needn't show every extreme that they name: The pairs (dest_device, dest_slot) name every row of the output exactly once. Each language-model shard receives exactly 128 tokens. At most 32 tokens of one source shard go to one language-model shard, and some pairs of shards reach 32. `dest_slot`: see dest_device.
All inputs are finite; a program needn't handle non-finite values.
Results may differ from the reference program's by a relative error of at most 0.0049.
Values may be sent and summed in bfloat16 or wider, within the bound.
A program may use at most 64 MiB of HBM per device.

```python
import jax
import jax.numpy as jnp
from jax import lax

D_IN = 1280
D = 3584
HEAD = 128
TOK_DEV = 128
NSRC = 8
TOKENS = 1024
BLOCK = 32
N_SEQ = 4
N_MDL = 2


def routing(key):
    base = jax.random.fold_in(key, 7)
    keys = jax.random.split(base, 4)
    shard_count = N_SEQ * N_MDL
    block_count = TOK_DEV // BLOCK
    inner_order = jax.random.permutation(keys[0], shard_count).astype(jnp.int32)
    outer_order = jax.random.permutation(keys[1], shard_count).astype(jnp.int32)
    shifts = jax.random.permutation(keys[2], shard_count).astype(jnp.int32)[:block_count]
    block_order = jax.random.permutation(keys[3], block_count).astype(jnp.int32)
    everyone = jnp.arange(TOKENS, dtype=jnp.int32)
    source = everyone // TOK_DEV
    within = everyone % TOK_DEV
    block_index = within // BLOCK
    inside = within % BLOCK
    device = outer_order[(inner_order[source] + shifts[block_index]) % shard_count]
    target = block_order[block_index] * BLOCK + inside
    return (device.astype(jnp.int32), target.astype(jnp.int32))


def draw_dest_device(key, part):
    return routing(key)[0]


def draw_dest_slot(key, part):
    return routing(key)[1]


def place_ends(result, stream_key, least, top_value):
    shape = result.shape
    index_at = [jax.random.randint(jax.random.fold_in(stream_key, axis), (), 0, shape[axis]) for axis in range(len(shape))]
    result = result.at[tuple(index_at)].set(least)
    longest = shape.index(max(shape))
    index_at[longest] = (index_at[longest] + 1) % shape[longest]
    return result.at[tuple(index_at)].set(top_value)


def steps_of(stream_key, shape, pieces, least, top_value):
    def one(dim, shards_of):
        steps = jax.random.uniform(jax.random.fold_in(jax.random.fold_in(stream_key, 6), dim), (shards_of,), jnp.float32, least / len(pieces), top_value / len(pieces))
        return jnp.repeat(jnp.exp(steps), shape[dim] // shards_of).reshape((-1,) + (1,) * (len(shape) - dim - 1))

    factor_of = one(*pieces[0])
    for cut in pieces[1:]:
        factor_of = factor_of * one(*cut)
    return factor_of


def normal_values(key, extent, width, reach, shards=(), held_as=jnp.bfloat16):
    result = width * jax.random.normal(key, extent, jnp.float32)
    if shards:
        result = result * steps_of(key, extent, shards, -0.22, 0.18)
    return jnp.clip(result, -reach, reach).astype(held_as)


def setup_inputs(seed: int = 0, part: int = 0) -> dict:
    seeds = jax.random.split(jax.random.key(seed), 10)
    own_keys = jax.random.split(jax.random.fold_in(seeds[9], part), 10)
    return {
        "frames": normal_values(own_keys[0], (TOKENS, D_IN), 1.0, 6.0, ((0, 8),)),
        "audio_count": place_ends(jax.random.randint(own_keys[1], (NSRC,), 1, TOK_DEV), jax.random.fold_in(own_keys[1], 1), 1, TOK_DEV - 1).astype(jnp.int32),
        "pos_ids": place_ends(jax.random.randint(own_keys[2], (3, TOKENS), 0, 4096), jax.random.fold_in(own_keys[2], 1), 0, 4095).astype(jnp.int32),
        "gain_audio": jnp.clip(1.0 + 0.18 * jax.random.normal(seeds[3], (D_IN,), jnp.float32), 0.1, 1.9),
        "gain_video": jnp.clip(1.0 + 0.18 * jax.random.normal(seeds[4], (D_IN,), jnp.float32), 0.1, 1.9),
        "audio_proj": normal_values(seeds[5], (D_IN, D), D_IN ** -0.5, 0.15625, ((0, 8), (1, 2))),
        "video_proj": normal_values(seeds[6], (D_IN, D), D_IN ** -0.5, 0.15625, ((0, 8), (1, 2))),
        "dest_device": draw_dest_device(jax.random.fold_in(jax.random.fold_in(seeds[9], part), 71), part),
        "dest_slot": draw_dest_slot(jax.random.fold_in(jax.random.fold_in(seeds[9], part), 71), part),
    }


def normalize(frames, audio_mask, gain_audio, gain_video):
    values = frames.astype(jnp.float32)
    mean_square = lax.optimization_barrier(jnp.mean(values * values, axis=-1, keepdims=True))
    row_gain = jnp.where(audio_mask[:, None], gain_audio[None, :], gain_video[None, :])
    return (values * lax.rsqrt(mean_square + 1e-06) * row_gain).astype(jnp.bfloat16)

def rotate(values, positions):
    tok_rows = values.shape[0]
    half_size = HEAD // 2
    pair_index = jnp.arange(half_size, dtype=jnp.int32)[None, :]
    chosen = jnp.where(pair_index < HEAD // 8, positions[0][:, None], jnp.where(pair_index < HEAD * 5 // 16, positions[1][:, None], positions[2][:, None]))
    exponent = -2.0 * jnp.arange(half_size).astype(jnp.float32) / HEAD
    inverse_freq = jnp.power(jnp.float32(1000000.0), exponent)
    angles = chosen.astype(jnp.float32) * inverse_freq[None, :]
    cosine = jnp.cos(angles)[:, None, :]
    sinus = jnp.sin(angles)[:, None, :]
    by_head = values.reshape(tok_rows, -1, HEAD)
    lower = by_head[:, :, :half_size]
    second = by_head[:, :, half_size:]
    turned = jnp.concatenate([lower * cosine - second * sinus, second * cosine + lower * sinus], axis=-1)
    return turned.reshape(tok_rows, -1)

def reference(frames, audio_count, pos_ids, gain_audio, gain_video, audio_proj, video_proj, dest_device, dest_slot):
    index_local = jnp.arange(TOK_DEV, dtype=jnp.int32)

    def one_source(inputs):
        source_rows, audio_rows, positions = inputs
        audio_mask = index_local < audio_rows
        normed = normalize(source_rows, audio_mask, gain_audio, gain_video)
        from_audio = jnp.dot(normed, audio_proj, preferred_element_type=jnp.float32)
        from_video = jnp.dot(normed, video_proj, preferred_element_type=jnp.float32)
        selected = jnp.where(audio_mask[:, None], from_audio, from_video)
        return rotate(selected, positions).astype(jnp.bfloat16)
    blocks = frames.reshape(NSRC, TOK_DEV, D_IN)
    positions = pos_ids.reshape(3, NSRC, TOK_DEV).transpose(1, 0, 2)
    embedded = lax.map(one_source, (blocks, audio_count, positions)).reshape(TOKENS, D)
    target = (dest_device * TOK_DEV + dest_slot).astype(jnp.int32)
    return jnp.zeros((TOKENS, D), jnp.bfloat16).at[target].set(embedded)
```

```python
import functools

import jax
import jax.numpy as jnp
from jax import lax
from jax.experimental import pallas as pl
from jax.experimental.pallas import tpu as pltpu
from jax.sharding import PartitionSpec as P

HEAD = 128
META = 16
MESH = pl.DeviceIdType.MESH


def normalize(frames, audio_mask, gain_audio, gain_video):
    values = frames.astype(jnp.float32)
    mean_square = jnp.mean(values * values, axis=-1, keepdims=True)
    row_gain = jnp.where(audio_mask[:, None], gain_audio[None, :], gain_video[None, :])
    return (values * lax.rsqrt(mean_square + 1e-06) * row_gain).astype(jnp.bfloat16)


def inverse_frequencies():
    exponent = -2.0 * jnp.arange(HEAD // 2).astype(jnp.float32) / HEAD
    return jnp.power(jnp.float32(1000000.0), exponent)


def rotate(values, positions):
    tok_rows = values.shape[0]
    half_size = HEAD // 2
    pair_index = jnp.arange(half_size, dtype=jnp.int32)[None, :]
    chosen = jnp.where(
        pair_index < HEAD // 8,
        positions[0][:, None],
        jnp.where(pair_index < HEAD * 5 // 16, positions[1][:, None], positions[2][:, None]),
    )
    angles = chosen.astype(jnp.float32) * inverse_frequencies()[None, :]
    cosine = jnp.cos(angles)[:, None, :]
    sinus = jnp.sin(angles)[:, None, :]
    by_head = values.reshape(tok_rows, -1, HEAD)
    lower = by_head[:, :, :half_size]
    second = by_head[:, :, half_size:]
    turned = jnp.concatenate(
        [lower * cosine - second * sinus, second * cosine + lower * sinus], axis=-1
    )
    return turned.reshape(tok_rows, -1)


def embed_rows(normed, audio_mask, positions, audio_proj, video_proj):
    from_audio = jnp.dot(
        normed,
        lax.all_gather(audio_proj, ("seq", "mdl"), axis=0, tiled=True),
        preferred_element_type=jnp.float32,
    )
    from_video = jnp.dot(
        normed,
        lax.all_gather(video_proj, ("seq", "mdl"), axis=0, tiled=True),
        preferred_element_type=jnp.float32,
    )
    selected = jnp.where(audio_mask[:, None], from_audio, from_video)
    return rotate(selected, positions).astype(jnp.bfloat16)


def gathered_plan(
    frames, audio_count, pos_ids, gain_audio, gain_video, audio_proj, video_proj, dest_device, dest_slot
):
    tok_rows = frames.shape[0]
    audio_mask = jnp.arange(tok_rows, dtype=jnp.int32) < audio_count[0]
    peer_count = lax.axis_size(("seq", "mdl"))
    capacity = 2 * tok_rows // peer_count
    onehot = (dest_device[:, None] == jnp.arange(peer_count, dtype=jnp.int32)[None, :]).astype(
        jnp.int32
    )
    arrival = jnp.sum(jnp.cumsum(onehot, axis=0) * onehot, axis=1) - 1
    bucket = dest_device * capacity + arrival
    normed = normalize(frames, audio_mask, gain_audio, gain_video)
    features = normed.shape[1]
    described = jnp.concatenate(
        [pos_ids.T, audio_mask.astype(jnp.int32)[:, None], dest_slot[:, None]], axis=1
    )
    outbox = jnp.zeros((peer_count * capacity, features), jnp.bfloat16).at[bucket].set(normed)
    blank_tags = jnp.concatenate(
        [
            jnp.zeros((peer_count * capacity, 4), jnp.int32),
            jnp.full((peer_count * capacity, 1), tok_rows, jnp.int32),
        ],
        axis=1,
    )
    tag_rows = blank_tags.at[bucket].set(described)
    received = lax.all_to_all(outbox, ("seq", "mdl"), split_axis=0, concat_axis=0, tiled=True)
    got_tags = lax.all_to_all(tag_rows, ("seq", "mdl"), split_axis=0, concat_axis=0, tiled=True)
    arrived = got_tags[:, 4]
    placed = jnp.zeros((tok_rows, features), jnp.bfloat16).at[arrived].set(received, mode="drop")
    placed_tags = jnp.zeros((tok_rows, 5), jnp.int32).at[arrived].set(got_tags, mode="drop")
    return embed_rows(placed, placed_tags[:, 3] > 0, placed_tags[:, :3].T, audio_proj, video_proj)


def kernel(
    n_seq,
    chunk,
    early,
    count_ref,
    frames_ref,
    pos_ref,
    dev_ref,
    slot_ref,
    gain_a_ref,
    gain_v_ref,
    freq_ref,
    audio_hbm,
    video_hbm,
    out_ref,
    xbuf,
    stage,
    meta,
    hot,
    lhs,
    weights,
    outbox,
    inbox,
    own,
    turn,
    x1_send,
    x1_recv,
    m1_send,
    m1_recv,
    x2_sem,
    m2_sem,
    x3_sem,
    w_send,
    w_recv,
    w_own,
    p_send,
    p_recv,
):
    z = lax.axis_index("seq")
    x = lax.axis_index("mdl")
    core = lax.axis_index("sub")
    tok, features = frames_ref.shape
    deep = audio_hbm.shape[0]
    width = features // n_seq
    chunks = audio_hbm.shape[1] // chunk
    part = tok // 2
    mine = pl.ds(pl.multiple_of(core * part, part), part)

    def seq_peer(step):
        return lax.rem(z + step, n_seq)

    barrier = pltpu.get_barrier_semaphore()
    for step in range(1, n_seq):
        pl.semaphore_signal(barrier, inc=1, device_id={"seq": seq_peer(step)}, device_id_type=MESH)
    pl.semaphore_signal(barrier, inc=1, device_id={"mdl": 1 - x}, device_id_type=MESH)
    pl.semaphore_signal(barrier, inc=1, device_id={"sub": 1 - core}, device_id_type=MESH)

    def weight_rows(kind):
        return pl.ds(pl.multiple_of(kind * width + x * deep, 16), deep)

    own_weights = [
        pltpu.make_async_copy(ref, weights.at[weight_rows(kind)], w_own.at[kind])
        for kind, ref in enumerate((audio_hbm, video_hbm))
    ]
    for copy in own_weights:
        copy.start()

    def weight_copy(kind, c):
        ref = (audio_hbm, video_hbm)[kind]
        cols = pl.ds(pl.multiple_of(c * chunk, chunk), chunk)
        return pltpu.make_async_remote_copy(
            src_ref=ref.at[:, cols],
            dst_ref=weights.at[weight_rows(kind), cols],
            send_sem=w_send.at[kind, c],
            recv_sem=w_recv.at[kind, c],
            device_id={"mdl": 1 - x},
            device_id_type=MESH,
        )

    def weight_arrival(kind, c):
        ref = (audio_hbm, video_hbm)[kind]
        cols = pl.ds(pl.multiple_of(c * chunk, chunk), chunk)
        rows = pl.ds(pl.multiple_of(kind * width + (1 - x) * deep, 16), deep)
        return pltpu.make_async_remote_copy(
            src_ref=ref.at[:, cols],
            dst_ref=weights.at[rows, cols],
            send_sem=w_send.at[kind, c],
            recv_sem=w_recv.at[kind, c],
            device_id={"mdl": 1 - x},
            device_id_type=MESH,
        )

    count = count_ref[0]
    values = frames_ref[mine, :].astype(jnp.float32)
    mean_square = jnp.mean(values * values, axis=-1, keepdims=True)
    token = lax.broadcasted_iota(jnp.int32, (part, features), 0) + core * part
    gain = jnp.where(token < count, gain_a_ref[...], gain_v_ref[...])
    normed = (values * lax.rsqrt(mean_square + 1e-06) * gain).astype(jnp.bfloat16)
    for target in range(n_seq):
        stage[target] = normed[:, target * width : (target + 1) * width]

    lane = lax.broadcasted_iota(jnp.int32, (META, tok), 1)
    row = lax.broadcasted_iota(jnp.int32, (META, tok), 0)
    device = dev_ref[...]
    target_seq = device // 2
    lines = [pos_ref[i : i + 1, :] >> 6 for i in range(3)]
    lines += [pos_ref[i : i + 1, :] & 63 for i in range(3)]
    lines += [jnp.where(lane[0:1, :] < count, 1, 0)]
    lines += [target_seq, device - target_seq * 2, slot_ref[...]]
    table = jnp.zeros((META, tok), jnp.int32)
    for i, line in enumerate(lines):
        table = jnp.where(row == i, line, table)
    meta[x, z] = table.astype(jnp.float32)

    pl.semaphore_wait(barrier, n_seq + 1)

    def x1_copy(step, source):
        return pltpu.make_async_remote_copy(
            src_ref=stage.at[seq_peer(step)],
            dst_ref=xbuf.at[x, source, mine],
            send_sem=x1_send.at[step],
            recv_sem=x1_recv.at[step],
            device_id={"seq": seq_peer(step)},
            device_id_type=MESH,
        )

    def m1_copy(step, source):
        return pltpu.make_async_remote_copy(
            src_ref=meta.at[x, z],
            dst_ref=meta.at[x, source],
            send_sem=m1_send.at[step],
            recv_sem=m1_recv.at[step],
            device_id={"seq": seq_peer(step)},
            device_id_type=MESH,
        )

    for step in range(1, n_seq):
        x1_copy(step, z).start()
        m1_copy(step, z).start()
    for c in range(early):
        for kind in range(2):
            weight_copy(kind, c).start()
    xbuf[x, z, mine, :] = stage[z]
    for step in range(1, n_seq):
        x1_copy(step, seq_peer(n_seq - step)).wait_recv()
        m1_copy(step, seq_peer(n_seq - step)).wait_recv()

    def x2_copy(column):
        return pltpu.make_async_remote_copy(
            src_ref=xbuf.at[x, :, mine],
            dst_ref=xbuf.at[column, :, mine],
            send_sem=x2_sem.at[0],
            recv_sem=x2_sem.at[1],
            device_id={"mdl": 1 - x},
            device_id_type=MESH,
        )

    def m2_copy(column):
        return pltpu.make_async_remote_copy(
            src_ref=meta.at[x],
            dst_ref=meta.at[column],
            send_sem=m2_sem.at[0],
            recv_sem=m2_sem.at[1],
            device_id={"mdl": 1 - x},
            device_id_type=MESH,
        )

    def x3_copy(column, half):
        rows = pl.ds(pl.multiple_of(half * part, part), part)
        return pltpu.make_async_remote_copy(
            src_ref=xbuf.at[column, :, mine],
            dst_ref=xbuf.at[column, :, rows],
            send_sem=x3_sem.at[0, column],
            recv_sem=x3_sem.at[1, column],
            device_id={"sub": 1 - core},
            device_id_type=MESH,
        )

    m2_copy(x).start()
    x2_copy(x).start()
    for c in range(early, chunks):
        for kind in range(2):
            weight_copy(kind, c).start()
    x3_copy(x, core).start()
    m2_copy(1 - x).wait_recv()

    rows = lax.broadcasted_iota(jnp.int32, (n_seq * tok, tok), 0)
    facts = jnp.zeros((n_seq * tok, META), jnp.float32)
    for k in range(2 * n_seq):
        about = meta[k // n_seq, k % n_seq]
        ints = about.astype(jnp.int32)
        ahead = ints[7:8, :] - z
        ahead = jnp.where(ahead < 0, ahead + n_seq, ahead)
        key = jnp.where(ints[8:9, :] == x, ahead * tok + ints[9:10, :], -1)
        piece = jnp.where(rows == key, 1.0, 0.0).astype(jnp.bfloat16)
        hot[:, k * tok : (k + 1) * tok] = piece
        facts += lax.dot_general(
            piece, about.astype(jnp.bfloat16), (((1,), (1,)), ((), ())), preferred_element_type=jnp.float32
        )

    lanes = lax.broadcasted_iota(jnp.int32, (tok, HEAD), 1)
    pair = jnp.where(lanes < HEAD // 2, lanes, lanes - HEAD // 2)
    place = [facts[:tok, i : i + 1] * 64.0 + facts[:tok, i + 3 : i + 4] for i in range(3)]
    chosen = jnp.where(pair < HEAD // 8, place[0], jnp.where(pair < HEAD * 5 // 16, place[1], place[2]))
    angles = chosen * freq_ref[...]
    turn[0] = jnp.cos(angles)
    sinus = jnp.sin(angles)
    turn[1] = jnp.where(lanes < HEAD // 2, -sinus, sinus)

    x2_copy(1 - x).wait_recv()
    x3_copy(1 - x, core).start()
    for column in range(2):
        x3_copy(column, 1 - core).wait_recv()

    everyone = xbuf[...].reshape(2 * n_seq * tok, width)
    sorted_rows = jnp.dot(hot[...], everyone, preferred_element_type=jnp.float32)
    is_audio = facts[:, 6:7] > 0.5
    lhs[:, :width] = jnp.where(is_audio, sorted_rows, 0.0).astype(jnp.bfloat16)
    lhs[:, width:] = jnp.where(is_audio, 0.0, sorted_rows).astype(jnp.bfloat16)

    for copy in own_weights:
        copy.wait()

    def part_copy(step, c):
        return pltpu.make_async_remote_copy(
            src_ref=outbox.at[step - 1, c],
            dst_ref=inbox.at[step - 1, c],
            send_sem=p_send.at[step - 1, c],
            recv_sem=p_recv.at[step - 1, c],
            device_id={"seq": seq_peer(step)},
            device_id_type=MESH,
        )

    def multiply(c, carry):
        for kind in range(2):
            weight_arrival(kind, c).wait_recv()
        cols = pl.ds(pl.multiple_of(c * chunk, chunk), chunk)
        product = jnp.dot(lhs[...], weights[:, cols], preferred_element_type=jnp.float32)
        for step in range(1, n_seq):
            outbox[step - 1, c] = product[step * tok : (step + 1) * tok, :].astype(jnp.bfloat16)
        for step in range(1, n_seq):
            part_copy(step, c).start()
        own[c] = product[:tok, :]
        return carry

    lax.fori_loop(0, chunks, multiply, 0)

    def finish(c, carry):
        for step in range(1, n_seq):
            part_copy(step, c).wait_recv()
        total = own[c]
        for step in range(1, n_seq):
            total += inbox[step - 1, c].astype(jnp.float32)
        for h in range(chunk // HEAD):
            head = total[:, h * HEAD : (h + 1) * HEAD]
            turned = head * turn[0] + pltpu.roll(head, HEAD // 2, 1) * turn[1]
            at = pl.ds(pl.multiple_of(c * chunk + h * HEAD, HEAD), HEAD)
            out_ref[:, at] = turned.astype(out_ref.dtype)
        return carry

    lax.fori_loop(0, chunks, finish, 0)

    for step in range(1, n_seq):
        x1_copy(step, z).wait_send()
        m1_copy(step, z).wait_send()
    x2_copy(x).wait_send()
    m2_copy(x).wait_send()
    for column in range(2):
        x3_copy(column, core).wait_send()

    def drain(c, carry):
        for kind in range(2):
            weight_copy(kind, c).wait_send()
        for step in range(1, n_seq):
            part_copy(step, c).wait_send()
        return carry

    lax.fori_loop(0, chunks, drain, 0)


def exchanged_plan(
    frames, audio_count, pos_ids, gain_audio, gain_video, audio_proj, video_proj, dest_device, dest_slot
):
    n_seq = lax.axis_size("seq")
    tok, features = frames.shape
    deep, columns = audio_proj.shape
    width = features // n_seq
    chunk = next(k for k in (2 * HEAD, HEAD) if columns % k == 0)
    chunks = columns // chunk
    early = min(2, chunks)
    freq = inverse_frequencies()
    freq = jnp.concatenate([freq, freq])[None, :]
    vmem = pl.BlockSpec(memory_space=pltpu.VMEM)
    smem = pl.BlockSpec(memory_space=pltpu.SMEM)
    anywhere = pl.BlockSpec(memory_space=pl.ANY)
    dma = pltpu.SemaphoreType.DMA
    bf16, f32 = jnp.bfloat16, jnp.float32
    return pl.pallas_call(
        functools.partial(kernel, n_seq, chunk, early),
        out_shape=jax.ShapeDtypeStruct((tok, columns), bf16),
        in_specs=[smem] + [vmem] * 7 + [anywhere] * 2,
        out_specs=vmem,
        scratch_shapes=[
            pltpu.VMEM((2, n_seq, tok, width), bf16),
            pltpu.VMEM((n_seq, tok // 2, width), bf16),
            pltpu.VMEM((2, n_seq, META, tok), f32),
            pltpu.VMEM((n_seq * tok, 2 * n_seq * tok), bf16),
            pltpu.VMEM((n_seq * tok, 2 * width), bf16),
            pltpu.VMEM((2 * width, columns), bf16),
            pltpu.VMEM((n_seq - 1, chunks, tok, chunk), bf16),
            pltpu.VMEM((n_seq - 1, chunks, tok, chunk), bf16),
            pltpu.VMEM((chunks, tok, chunk), f32),
            pltpu.VMEM((2, tok, HEAD), f32),
            dma((n_seq,)),
            dma((n_seq,)),
            dma((n_seq,)),
            dma((n_seq,)),
            dma((2,)),
            dma((2,)),
            dma((2, 2)),
            dma((2, chunks)),
            dma((2, chunks)),
            dma((2,)),
            dma((n_seq - 1, chunks)),
            dma((n_seq - 1, chunks)),
        ],
        compiler_params=pltpu.CompilerParams(
            collective_id=0, has_side_effects=True, vmem_limit_bytes=48 * 1024 * 1024
        ),
    )(
        audio_count,
        frames,
        pos_ids,
        dest_device[None, :],
        dest_slot[None, :],
        gain_audio[None, :],
        gain_video[None, :],
        freq,
        audio_proj,
        video_proj,
    )


def solution(mesh):
    in_specs = (
        P(("grp", "seq", "mdl"), None),
        P(("grp", "seq", "mdl")),
        P(None, ("grp", "seq", "mdl")),
        P(),
        P(),
        P(("seq", "mdl"), "sub"),
        P(("seq", "mdl"), "sub"),
        P(("grp", "seq", "mdl")),
        P(("grp", "seq", "mdl")),
    )
    out_specs = P(("grp", "seq", "mdl"), "sub")
    paired = mesh.shape["mdl"] == 2 and mesh.shape["sub"] == 2
    plan = exchanged_plan if paired else gathered_plan
    return jax.shard_map(plan, mesh=mesh, in_specs=in_specs, out_specs=out_specs, check_vma=False)
```

```python
import functools

import jax
import jax.numpy as jnp
from jax import lax
from jax.experimental import pallas as pl
from jax.experimental.pallas import tpu as pltpu
from jax.sharding import PartitionSpec as P

HEAD = 128
META = 16
MESH = pl.DeviceIdType.MESH


def normalize(frames, audio_mask, gain_audio, gain_video):
    values = frames.astype(jnp.float32)
    mean_square = jnp.mean(values * values, axis=-1, keepdims=True)
    row_gain = jnp.where(audio_mask[:, None], gain_audio[None, :], gain_video[None, :])
    return (values * lax.rsqrt(mean_square + 1e-06) * row_gain).astype(jnp.bfloat16)


def inverse_frequencies():
    exponent = -2.0 * jnp.arange(HEAD // 2).astype(jnp.float32) / HEAD
    return jnp.power(jnp.float32(1000000.0), exponent)


def rotate(values, positions):
    tok_rows = values.shape[0]
    half_size = HEAD // 2
    pair_index = jnp.arange(half_size, dtype=jnp.int32)[None, :]
    chosen = jnp.where(
        pair_index < HEAD // 8,
        positions[0][:, None],
        jnp.where(pair_index < HEAD * 5 // 16, positions[1][:, None], positions[2][:, None]),
    )
    angles = chosen.astype(jnp.float32) * inverse_frequencies()[None, :]
    cosine = jnp.cos(angles)[:, None, :]
    sinus = jnp.sin(angles)[:, None, :]
    by_head = values.reshape(tok_rows, -1, HEAD)
    lower = by_head[:, :, :half_size]
    second = by_head[:, :, half_size:]
    turned = jnp.concatenate(
        [lower * cosine - second * sinus, second * cosine + lower * sinus], axis=-1
    )
    return turned.reshape(tok_rows, -1)


def embed_rows(normed, audio_mask, positions, audio_proj, video_proj):
    from_audio = jnp.dot(
        normed,
        lax.all_gather(audio_proj, ("seq", "mdl"), axis=0, tiled=True),
        preferred_element_type=jnp.float32,
    )
    from_video = jnp.dot(
        normed,
        lax.all_gather(video_proj, ("seq", "mdl"), axis=0, tiled=True),
        preferred_element_type=jnp.float32,
    )
    selected = jnp.where(audio_mask[:, None], from_audio, from_video)
    return rotate(selected, positions).astype(jnp.bfloat16)


def gathered_plan(
    frames, audio_count, pos_ids, gain_audio, gain_video, audio_proj, video_proj, dest_device, dest_slot
):
    tok_rows = frames.shape[0]
    audio_mask = jnp.arange(tok_rows, dtype=jnp.int32) < audio_count[0]
    peer_count = lax.axis_size(("seq", "mdl"))
    capacity = 2 * tok_rows // peer_count
    onehot = (dest_device[:, None] == jnp.arange(peer_count, dtype=jnp.int32)[None, :]).astype(
        jnp.int32
    )
    arrival = jnp.sum(jnp.cumsum(onehot, axis=0) * onehot, axis=1) - 1
    bucket = dest_device * capacity + arrival
    normed = normalize(frames, audio_mask, gain_audio, gain_video)
    features = normed.shape[1]
    described = jnp.concatenate(
        [pos_ids.T, audio_mask.astype(jnp.int32)[:, None], dest_slot[:, None]], axis=1
    )
    outbox = jnp.zeros((peer_count * capacity, features), jnp.bfloat16).at[bucket].set(normed)
    blank_tags = jnp.concatenate(
        [
            jnp.zeros((peer_count * capacity, 4), jnp.int32),
            jnp.full((peer_count * capacity, 1), tok_rows, jnp.int32),
        ],
        axis=1,
    )
    tag_rows = blank_tags.at[bucket].set(described)
    received = lax.all_to_all(outbox, ("seq", "mdl"), split_axis=0, concat_axis=0, tiled=True)
    got_tags = lax.all_to_all(tag_rows, ("seq", "mdl"), split_axis=0, concat_axis=0, tiled=True)
    arrived = got_tags[:, 4]
    placed = jnp.zeros((tok_rows, features), jnp.bfloat16).at[arrived].set(received, mode="drop")
    placed_tags = jnp.zeros((tok_rows, 5), jnp.int32).at[arrived].set(got_tags, mode="drop")
    return embed_rows(placed, placed_tags[:, 3] > 0, placed_tags[:, :3].T, audio_proj, video_proj)


def kernel(
    chunk,
    early,
    count_hbm,
    frames_hbm,
    pos_hbm,
    dev_hbm,
    slot_hbm,
    gain_a_hbm,
    gain_v_hbm,
    freq_ref,
    audio_hbm,
    video_hbm,
    out_ref,
    count_ref,
    frames_ref,
    pos_ref,
    dev_ref,
    slot_ref,
    gain_a_ref,
    gain_v_ref,
    xbuf,
    stage,
    meta,
    hot,
    lhs,
    weights,
    outbox,
    inbox,
    own,
    far,
    turn,
    in_sem,
    x1_send,
    x1_recv,
    m1_send,
    m1_recv,
    x2_send,
    x2_recv,
    m2_send,
    m2_recv,
    x3_send,
    x3_recv,
    w_send,
    w_recv,
    w_own,
    p_send,
    p_recv,
):
    n_seq = 4
    z = lax.axis_index("seq")
    x = lax.axis_index("mdl")
    core = lax.axis_index("sub")
    features = frames_hbm.shape[1]
    tok = frames_hbm.shape[0]
    deep = audio_hbm.shape[0]
    width = features // n_seq
    chunks = audio_hbm.shape[1] // chunk
    part = tok // 2
    mine = pl.ds(pl.multiple_of(core * part, part), part)
    inner = jnp.logical_or(z == 1, z == 2)
    peers = (z, z + 1 - 2 * lax.rem(z, 2), lax.rem(z + 2, n_seq), n_seq - 1 - z)

    loads = [
        pltpu.make_async_copy(src, dst, in_sem.at[i])
        for i, (src, dst) in enumerate(
            (
                (frames_hbm.at[mine], frames_ref),
                (gain_a_hbm, gain_a_ref),
                (gain_v_hbm, gain_v_ref),
                (count_hbm, count_ref),
                (pos_hbm, pos_ref),
                (dev_hbm, dev_ref),
                (slot_hbm, slot_ref),
            )
        )
    ]
    for copy in loads:
        copy.start()

    barrier = pltpu.get_barrier_semaphore()
    for q in range(1, n_seq):
        pl.semaphore_signal(barrier, inc=1, device_id={"seq": peers[q]}, device_id_type=MESH)
    pl.semaphore_signal(barrier, inc=1, device_id={"mdl": 1 - x}, device_id_type=MESH)
    pl.semaphore_signal(barrier, inc=1, device_id={"sub": 1 - core}, device_id_type=MESH)

    def weight_rows(kind, column):
        return pl.ds(pl.multiple_of(kind * width + column * deep, 16), deep)

    own_weights = [
        pltpu.make_async_copy(ref, weights.at[weight_rows(kind, x)], w_own.at[kind])
        for kind, ref in enumerate((audio_hbm, video_hbm))
    ]
    for copy in own_weights:
        copy.start()

    def weight_copy(kind, c, column):
        cols = pl.ds(pl.multiple_of(c * chunk, chunk), chunk)
        return pltpu.make_async_remote_copy(
            src_ref=(audio_hbm, video_hbm)[kind].at[:, cols],
            dst_ref=weights.at[weight_rows(kind, column), cols],
            send_sem=w_send.at[kind, c],
            recv_sem=w_recv.at[kind, c],
            device_id={"mdl": 1 - x},
            device_id_type=MESH,
        )

    for copy in loads:
        copy.wait()
    count = count_ref[0]
    lane = lax.broadcasted_iota(jnp.int32, (META, tok), 1)
    row = lax.broadcasted_iota(jnp.int32, (META, tok), 0)
    device = dev_ref[...]
    target_seq = device // 2
    lines = [pos_ref[i : i + 1, :] >> 6 for i in range(3)]
    lines += [pos_ref[i : i + 1, :] & 63 for i in range(3)]
    lines += [jnp.where(lane[0:1, :] < count, 1, 0)]
    lines += [target_seq, device - target_seq * 2, slot_ref[...]]
    table = jnp.zeros((META, tok), jnp.int32)
    for i, line in enumerate(lines):
        table = jnp.where(row == i, line, table)
    meta[x, z] = table.astype(jnp.float32)

    values = frames_ref[...].astype(jnp.float32)
    mean_square = jnp.mean(values * values, axis=-1, keepdims=True)
    token = lax.broadcasted_iota(jnp.int32, (part, features), 0) + core * part
    gain = jnp.where(token < count, gain_a_ref[...], gain_v_ref[...])
    normed = (values * lax.rsqrt(mean_square + 1e-06) * gain).astype(jnp.bfloat16)
    for target in range(n_seq):
        stage[target] = normed[:, target * width : (target + 1) * width]
    xbuf[x, z, mine, :] = stage[z]

    pl.semaphore_wait(barrier, n_seq + 1)

    def x1_copy(q, source):
        return pltpu.make_async_remote_copy(
            src_ref=stage.at[peers[q]],
            dst_ref=xbuf.at[x, source, mine],
            send_sem=x1_send.at[q],
            recv_sem=x1_recv.at[q],
            device_id={"seq": peers[q]},
            device_id_type=MESH,
        )

    def m1_copy(q, source):
        return pltpu.make_async_remote_copy(
            src_ref=meta.at[x, z],
            dst_ref=meta.at[x, source],
            send_sem=m1_send.at[q],
            recv_sem=m1_recv.at[q],
            device_id={"seq": peers[q]},
            device_id_type=MESH,
        )

    def x2_copy(q, column):
        return pltpu.make_async_remote_copy(
            src_ref=xbuf.at[x, peers[q], mine],
            dst_ref=xbuf.at[column, peers[q], mine],
            send_sem=x2_send.at[q],
            recv_sem=x2_recv.at[q],
            device_id={"mdl": 1 - x},
            device_id_type=MESH,
        )

    def m2_copy(q, column):
        return pltpu.make_async_remote_copy(
            src_ref=meta.at[x, peers[q]],
            dst_ref=meta.at[column, peers[q]],
            send_sem=m2_send.at[q],
            recv_sem=m2_recv.at[q],
            device_id={"mdl": 1 - x},
            device_id_type=MESH,
        )

    def x3_copy(q, column, half, slot):
        rows = pl.ds(pl.multiple_of(half * part, part), part)
        return pltpu.make_async_remote_copy(
            src_ref=xbuf.at[column, peers[q], mine],
            dst_ref=xbuf.at[column, peers[q], rows],
            send_sem=x3_send.at[slot, q],
            recv_sem=x3_recv.at[slot, q],
            device_id={"sub": 1 - core},
            device_id_type=MESH,
        )

    for q in range(n_seq - 1, 0, -1):
        m1_copy(q, z).start()
        x1_copy(q, z).start()
    m2_copy(0, x).start()
    x2_copy(0, x).start()
    for c in range(early):
        for kind in range(2):
            weight_copy(kind, c, x).start()
    x3_copy(0, x, core, 0).start()

    rows = lax.broadcasted_iota(jnp.int32, (n_seq * tok, tok), 0)

    def place(column, q):
        about = meta[column, peers[q]]
        ints = about.astype(jnp.int32)
        block = jnp.bitwise_xor(ints[7:8, :], z)
        key = jnp.where(ints[8:9, :] == x, block * tok + ints[9:10, :], -1)
        piece = jnp.where(rows == key, 1.0, 0.0).astype(jnp.bfloat16)
        return piece, lax.dot_general(
            piece, about.astype(jnp.bfloat16), (((1,), (1,)), ((), ())), preferred_element_type=jnp.float32
        )

    piece, facts = place(x, 0)
    hot[:, :tok] = piece
    for q in range(1, n_seq):
        m1_copy(q, peers[q]).wait_recv()
        m2_copy(q, x).start()
        piece, more = place(x, q)
        hot[:, q * tok : (q + 1) * tok] = piece
        facts += more
    for q in range(1, n_seq):
        x1_copy(q, peers[q]).wait_recv()
        x2_copy(q, x).start()
        x3_copy(q, x, core, 0).start()
    for c in range(early, chunks):
        for kind in range(2):
            weight_copy(kind, c, x).start()
    for q in range(n_seq):
        m2_copy(q, 1 - x).wait_recv()
        piece, more = place(1 - x, q)
        hot[:, (n_seq + q) * tok : (n_seq + q + 1) * tok] = piece
        facts += more
    for q in range(n_seq):
        x2_copy(q, 1 - x).wait_recv()
        x3_copy(q, 1 - x, core, 1).start()
    for slot, column in enumerate((x, 1 - x)):
        for q in range(n_seq):
            x3_copy(q, column, 1 - core, slot).wait_recv()

    everyone = jnp.concatenate(
        [xbuf[column, peers[q]] for column in (x, 1 - x) for q in range(n_seq)], axis=0
    )
    sorted_rows = jnp.dot(hot[...], everyone, preferred_element_type=jnp.float32)
    is_audio = facts[:, 6:7] > 0.5
    lhs[:, :width] = jnp.where(is_audio, sorted_rows, 0.0).astype(jnp.bfloat16)
    lhs[:, width:] = jnp.where(is_audio, 0.0, sorted_rows).astype(jnp.bfloat16)

    for copy in own_weights:
        copy.wait()

    def part_copy(out_slot, in_slot, c, peer):
        return pltpu.make_async_remote_copy(
            src_ref=outbox.at[out_slot, c],
            dst_ref=inbox.at[in_slot, c],
            send_sem=p_send.at[out_slot, c],
            recv_sem=p_recv.at[in_slot, c],
            device_id={"seq": peer},
            device_id_type=MESH,
        )

    def relay(c):
        part_copy(2, 3, c, peers[1]).wait_recv()
        outbox[1, c] = (far[c] + inbox[3, c].astype(jnp.float32)).astype(jnp.bfloat16)
        part_copy(1, 1, c, peers[2]).start()

    def multiply(c, carry):
        for kind in range(2):
            weight_copy(kind, c, 1 - x).wait_recv()
        cols = pl.ds(pl.multiple_of(c * chunk, chunk), chunk)
        product = jnp.dot(lhs[...], weights[:, cols], preferred_element_type=jnp.float32)
        outbox[0, c] = product[tok : 2 * tok, :].astype(jnp.bfloat16)
        outbox[2, c] = product[3 * tok :, :].astype(jnp.bfloat16)

        @pl.when(jnp.logical_not(inner))
        def _():
            part_copy(2, 3, c, peers[1]).start()
            outbox[1, c] = product[2 * tok : 3 * tok, :].astype(jnp.bfloat16)
            part_copy(1, 1, c, peers[2]).start()
            part_copy(0, 0, c, peers[1]).start()

        @pl.when(inner)
        def _():
            part_copy(2, 2, c, peers[3]).start()
            part_copy(0, 0, c, peers[1]).start()
            far[c] = product[2 * tok : 3 * tok, :]

            @pl.when(c > 0)
            def _():
                relay(c - 1)

        own[c] = product[:tok, :]
        return carry

    lax.fori_loop(0, chunks, multiply, 0)

    lanes = lax.broadcasted_iota(jnp.int32, (tok, HEAD), 1)
    pair = jnp.where(lanes < HEAD // 2, lanes, lanes - HEAD // 2)
    at = [facts[:tok, i : i + 1] * 64.0 + facts[:tok, i + 3 : i + 4] for i in range(3)]
    chosen = jnp.where(pair < HEAD // 8, at[0], jnp.where(pair < HEAD * 5 // 16, at[1], at[2]))
    angles = chosen * freq_ref[...]
    turn[0] = jnp.cos(angles)
    sinus = jnp.sin(angles)
    turn[1] = jnp.where(lanes < HEAD // 2, -sinus, sinus)

    @pl.when(inner)
    def _():
        relay(chunks - 1)

    def finish(c, carry):
        part_copy(0, 0, c, peers[1]).wait_recv()
        part_copy(1, 1, c, peers[2]).wait_recv()

        @pl.when(inner)
        def _():
            part_copy(2, 2, c, peers[3]).wait_recv()
            own[c] = own[c] + inbox[2, c].astype(jnp.float32)

        total = own[c] + inbox[0, c].astype(jnp.float32) + inbox[1, c].astype(jnp.float32)
        for h in range(chunk // HEAD):
            head = total[:, h * HEAD : (h + 1) * HEAD]
            turned = head * turn[0] + pltpu.roll(head, HEAD // 2, 1) * turn[1]
            cols = pl.ds(pl.multiple_of(c * chunk + h * HEAD, HEAD), HEAD)
            out_ref[:, cols] = turned.astype(out_ref.dtype)
        return carry

    lax.fori_loop(0, chunks, finish, 0)

    for q in range(n_seq):
        if q:
            x1_copy(q, z).wait_send()
            m1_copy(q, z).wait_send()
        x2_copy(q, x).wait_send()
        m2_copy(q, x).wait_send()
        x3_copy(q, x, core, 0).wait_send()
        x3_copy(q, 1 - x, core, 1).wait_send()

    def drain(c, carry):
        for kind in range(2):
            weight_copy(kind, c, x).wait_send()
        for slot in range(3):
            part_copy(slot, slot, c, peers[1]).wait_send()
        return carry

    lax.fori_loop(0, chunks, drain, 0)


def exchanged_plan(
    frames, audio_count, pos_ids, gain_audio, gain_video, audio_proj, video_proj, dest_device, dest_slot
):
    n_seq = lax.axis_size("seq")
    tok, features = frames.shape
    deep, columns = audio_proj.shape
    width = features // n_seq
    chunk = next(k for k in (2 * HEAD, HEAD) if columns % k == 0)
    chunks = columns // chunk
    early = min(1, chunks)
    freq = inverse_frequencies()
    freq = jnp.concatenate([freq, freq])[None, :]
    vmem = pl.BlockSpec(memory_space=pltpu.VMEM)
    anywhere = pl.BlockSpec(memory_space=pl.ANY)
    dma = pltpu.SemaphoreType.DMA
    bf16, f32, i32 = jnp.bfloat16, jnp.float32, jnp.int32
    return pl.pallas_call(
        functools.partial(kernel, chunk, early),
        out_shape=jax.ShapeDtypeStruct((tok, columns), bf16),
        in_specs=[anywhere] * 7 + [vmem] + [anywhere] * 2,
        out_specs=vmem,
        scratch_shapes=[
            pltpu.SMEM((1,), i32),
            pltpu.VMEM((tok // 2, features), bf16),
            pltpu.VMEM((3, tok), i32),
            pltpu.VMEM((1, tok), i32),
            pltpu.VMEM((1, tok), i32),
            pltpu.VMEM((1, features), f32),
            pltpu.VMEM((1, features), f32),
            pltpu.VMEM((2, n_seq, tok, width), bf16),
            pltpu.VMEM((n_seq, tok // 2, width), bf16),
            pltpu.VMEM((2, n_seq, META, tok), f32),
            pltpu.VMEM((n_seq * tok, 2 * n_seq * tok), bf16),
            pltpu.VMEM((n_seq * tok, 2 * width), bf16),
            pltpu.VMEM((2 * width, columns), bf16),
            pltpu.VMEM((3, chunks, tok, chunk), bf16),
            pltpu.VMEM((4, chunks, tok, chunk), bf16),
            pltpu.VMEM((chunks, tok, chunk), f32),
            pltpu.VMEM((chunks, tok, chunk), f32),
            pltpu.VMEM((2, tok, HEAD), f32),
            dma((7,)),
        ]
        + [dma((n_seq,))] * 8
        + [dma((2, n_seq))] * 2
        + [dma((2, chunks))] * 2
        + [dma((2,)), dma((3, chunks)), dma((4, chunks))],
        compiler_params=pltpu.CompilerParams(
            collective_id=0, has_side_effects=True, vmem_limit_bytes=60 * 1024 * 1024
        ),
    )(
        audio_count,
        frames,
        pos_ids,
        dest_device[None, :],
        dest_slot[None, :],
        gain_audio[None, :],
        gain_video[None, :],
        freq,
        audio_proj,
        video_proj,
    )


def solution(mesh):
    in_specs = (
        P(("grp", "seq", "mdl"), None),
        P(("grp", "seq", "mdl")),
        P(None, ("grp", "seq", "mdl")),
        P(),
        P(),
        P(("seq", "mdl"), "sub"),
        P(("seq", "mdl"), "sub"),
        P(("grp", "seq", "mdl")),
        P(("grp", "seq", "mdl")),
    )
    out_specs = P(("grp", "seq", "mdl"), "sub")
    paired = (mesh.shape["seq"], mesh.shape["mdl"], mesh.shape["sub"]) == (4, 2, 2)
    plan = exchanged_plan if paired else gathered_plan
    return jax.shard_map(plan, mesh=mesh, in_specs=in_specs, out_specs=out_specs, check_vma=False)
```

```python
import functools
import math

import jax
import jax.numpy as jnp
from jax import lax
from jax.experimental import pallas as pl
from jax.experimental.pallas import tpu as pltpu
from jax.sharding import PartitionSpec as P

HEAD = 128
META = 16
MESH = pl.DeviceIdType.MESH


def normalize(frames, audio_mask, gain_audio, gain_video):
    values = frames.astype(jnp.float32)
    mean_square = jnp.mean(values * values, axis=-1, keepdims=True)
    row_gain = jnp.where(audio_mask[:, None], gain_audio[None, :], gain_video[None, :])
    return (values * lax.rsqrt(mean_square + 1e-06) * row_gain).astype(jnp.bfloat16)


def inverse_frequencies():
    exponent = -2.0 * jnp.arange(HEAD // 2).astype(jnp.float32) / HEAD
    return jnp.power(jnp.float32(1000000.0), exponent)


def rotate(values, positions):
    tok_rows = values.shape[0]
    half_size = HEAD // 2
    pair_index = jnp.arange(half_size, dtype=jnp.int32)[None, :]
    chosen = jnp.where(
        pair_index < HEAD // 8,
        positions[0][:, None],
        jnp.where(pair_index < HEAD * 5 // 16, positions[1][:, None], positions[2][:, None]),
    )
    angles = chosen.astype(jnp.float32) * inverse_frequencies()[None, :]
    cosine = jnp.cos(angles)[:, None, :]
    sinus = jnp.sin(angles)[:, None, :]
    by_head = values.reshape(tok_rows, -1, HEAD)
    lower = by_head[:, :, :half_size]
    second = by_head[:, :, half_size:]
    turned = jnp.concatenate(
        [lower * cosine - second * sinus, second * cosine + lower * sinus], axis=-1
    )
    return turned.reshape(tok_rows, -1)


def embed_rows(normed, audio_mask, positions, audio_proj, video_proj):
    from_audio = jnp.dot(
        normed,
        lax.all_gather(audio_proj, ("seq", "mdl"), axis=0, tiled=True),
        preferred_element_type=jnp.float32,
    )
    from_video = jnp.dot(
        normed,
        lax.all_gather(video_proj, ("seq", "mdl"), axis=0, tiled=True),
        preferred_element_type=jnp.float32,
    )
    selected = jnp.where(audio_mask[:, None], from_audio, from_video)
    return rotate(selected, positions).astype(jnp.bfloat16)


def gathered_plan(
    frames, audio_count, pos_ids, gain_audio, gain_video, audio_proj, video_proj, dest_device, dest_slot
):
    tok_rows = frames.shape[0]
    audio_mask = jnp.arange(tok_rows, dtype=jnp.int32) < audio_count[0]
    peer_count = lax.axis_size(("seq", "mdl"))
    capacity = 2 * tok_rows // peer_count
    onehot = (dest_device[:, None] == jnp.arange(peer_count, dtype=jnp.int32)[None, :]).astype(
        jnp.int32
    )
    arrival = jnp.sum(jnp.cumsum(onehot, axis=0) * onehot, axis=1) - 1
    bucket = dest_device * capacity + arrival
    normed = normalize(frames, audio_mask, gain_audio, gain_video)
    features = normed.shape[1]
    described = jnp.concatenate(
        [pos_ids.T, audio_mask.astype(jnp.int32)[:, None], dest_slot[:, None]], axis=1
    )
    outbox = jnp.zeros((peer_count * capacity, features), jnp.bfloat16).at[bucket].set(normed)
    blank_tags = jnp.concatenate(
        [
            jnp.zeros((peer_count * capacity, 4), jnp.int32),
            jnp.full((peer_count * capacity, 1), tok_rows, jnp.int32),
        ],
        axis=1,
    )
    tag_rows = blank_tags.at[bucket].set(described)
    received = lax.all_to_all(outbox, ("seq", "mdl"), split_axis=0, concat_axis=0, tiled=True)
    got_tags = lax.all_to_all(tag_rows, ("seq", "mdl"), split_axis=0, concat_axis=0, tiled=True)
    arrived = got_tags[:, 4]
    placed = jnp.zeros((tok_rows, features), jnp.bfloat16).at[arrived].set(received, mode="drop")
    placed_tags = jnp.zeros((tok_rows, 5), jnp.int32).at[arrived].set(got_tags, mode="drop")
    return embed_rows(placed, placed_tags[:, 3] > 0, placed_tags[:, :3].T, audio_proj, video_proj)


def kernel(
    chunk,
    early,
    count_hbm,
    frames_hbm,
    pos_hbm,
    dev_hbm,
    slot_hbm,
    gain_a_hbm,
    gain_v_hbm,
    audio_hbm,
    video_hbm,
    out_ref,
    count_ref,
    frames_ref,
    pos_ref,
    dev_ref,
    slot_ref,
    gain_a_ref,
    gain_v_ref,
    xbuf,
    stage,
    meta,
    hot,
    lhs,
    weights,
    outbox,
    inbox,
    own,
    far,
    turn,
    in_sem,
    x1_send,
    x1_recv,
    m1_send,
    m1_recv,
    x2_send,
    x2_recv,
    m2_send,
    m2_recv,
    x3_send,
    x3_recv,
    w_send,
    w_recv,
    w_own,
    p_send,
    p_recv,
):
    n_seq = 4
    z = lax.axis_index("seq")
    x = lax.axis_index("mdl")
    core = lax.axis_index("sub")
    group = lax.axis_index("grp")
    features = frames_hbm.shape[1]
    tok = frames_hbm.shape[0]
    deep = audio_hbm.shape[0]
    width = features // n_seq
    chunks = audio_hbm.shape[1] // chunk
    part = tok // 2
    mine = pl.ds(pl.multiple_of(core * part, part), part)
    inner = jnp.logical_or(z == 1, z == 2)
    peers = (z, z + 1 - 2 * lax.rem(z, 2), lax.rem(z + 2, n_seq), n_seq - 1 - z)

    loads = [
        pltpu.make_async_copy(src, dst, in_sem.at[i])
        for i, (src, dst) in enumerate(
            (
                (frames_hbm.at[mine], frames_ref),
                (gain_a_hbm, gain_a_ref),
                (gain_v_hbm, gain_v_ref),
                (count_hbm, count_ref),
                (pos_hbm, pos_ref),
                (dev_hbm, dev_ref),
                (slot_hbm, slot_ref),
            )
        )
    ]
    for copy in loads:
        copy.start()

    barrier = pltpu.get_barrier_semaphore()
    for q in range(1, n_seq):
        pl.semaphore_signal(barrier, inc=1, device_id={"seq": peers[q]}, device_id_type=MESH)
    pl.semaphore_signal(barrier, inc=1, device_id={"mdl": 1 - x}, device_id_type=MESH)
    pl.semaphore_signal(barrier, inc=1, device_id={"sub": 1 - core}, device_id_type=MESH)
    pl.semaphore_signal(barrier, inc=1, device_id={"grp": 1 - group}, device_id_type=MESH)

    def weight_rows(kind, column):
        return pl.ds(pl.multiple_of(kind * width + column * deep, 16), deep)

    own_weights = [
        pltpu.make_async_copy(ref, weights.at[weight_rows(kind, x)], w_own.at[kind])
        for kind, ref in enumerate((audio_hbm, video_hbm))
    ]
    for copy in own_weights:
        copy.start()

    def weight_copy(c, column):
        at = weights.at[weight_rows(group, column), pl.ds(pl.multiple_of(c * chunk, chunk), chunk)]
        return pltpu.make_async_remote_copy(
            src_ref=weights.at[weight_rows(group, x), pl.ds(pl.multiple_of(c * chunk, chunk), chunk)],
            dst_ref=at,
            send_sem=w_send.at[0, c],
            recv_sem=w_recv.at[0, c],
            device_id={"mdl": 1 - x},
            device_id_type=MESH,
        )

    def weight_pass(c, kind):
        cols = pl.ds(pl.multiple_of(c * chunk, chunk), chunk)
        return pltpu.make_async_remote_copy(
            src_ref=weights.at[weight_rows(group, 1 - x), cols],
            dst_ref=weights.at[weight_rows(kind, 1 - x), cols],
            send_sem=w_send.at[1, c],
            recv_sem=w_recv.at[1, c],
            device_id={"grp": 1 - group},
            device_id_type=MESH,
        )

    def start_weights(first, last):
        def start(c, carry):
            weight_copy(c, x).start()
            return carry

        lax.fori_loop(first, last, start, 0)

    def pass_weights(first, last):
        def forward(c, carry):
            weight_copy(c, 1 - x).wait_recv()
            weight_pass(c, group).start()
            return carry

        lax.fori_loop(first, last, forward, 0)

    def x1_copy(q, source):
        return pltpu.make_async_remote_copy(
            src_ref=stage.at[peers[q]],
            dst_ref=xbuf.at[x, source, mine],
            send_sem=x1_send.at[q],
            recv_sem=x1_recv.at[q],
            device_id={"seq": peers[q]},
            device_id_type=MESH,
        )

    def m1_copy(q, source):
        return pltpu.make_async_remote_copy(
            src_ref=meta.at[x, z],
            dst_ref=meta.at[x, source],
            send_sem=m1_send.at[q],
            recv_sem=m1_recv.at[q],
            device_id={"seq": peers[q]},
            device_id_type=MESH,
        )

    def x2_copy(q, column):
        return pltpu.make_async_remote_copy(
            src_ref=xbuf.at[x, peers[q], mine],
            dst_ref=xbuf.at[column, peers[q], mine],
            send_sem=x2_send.at[q],
            recv_sem=x2_recv.at[q],
            device_id={"mdl": 1 - x},
            device_id_type=MESH,
        )

    def m2_copy(q, column):
        return pltpu.make_async_remote_copy(
            src_ref=meta.at[x, peers[q]],
            dst_ref=meta.at[column, peers[q]],
            send_sem=m2_send.at[q],
            recv_sem=m2_recv.at[q],
            device_id={"mdl": 1 - x},
            device_id_type=MESH,
        )

    def x3_copy(q, column, half, slot):
        rows = pl.ds(pl.multiple_of(half * part, part), part)
        return pltpu.make_async_remote_copy(
            src_ref=xbuf.at[column, peers[q], mine],
            dst_ref=xbuf.at[column, peers[q], rows],
            send_sem=x3_send.at[slot, q],
            recv_sem=x3_recv.at[slot, q],
            device_id={"sub": 1 - core},
            device_id_type=MESH,
        )

    for copy in loads[3:]:
        copy.wait()
    count = count_ref[0]
    lane = lax.broadcasted_iota(jnp.int32, (META, tok), 1)
    row = lax.broadcasted_iota(jnp.int32, (META, tok), 0)
    device = dev_ref[...]
    target_seq = device // 2
    lines = [pos_ref[i : i + 1, :] >> 6 for i in range(3)]
    lines += [pos_ref[i : i + 1, :] & 63 for i in range(3)]
    lines += [jnp.where(lane[0:1, :] < count, 1, 0)]
    lines += [target_seq, device - target_seq * 2, slot_ref[...]]
    table = jnp.zeros((META, tok), jnp.int32)
    for i, line in enumerate(lines):
        table = jnp.where(row == i, line, table)
    meta[x, z] = table.astype(jnp.float32)

    pl.semaphore_wait(barrier, n_seq + 2)
    for q in range(n_seq - 1, 0, -1):
        m1_copy(q, z).start()
    m2_copy(0, x).start()

    for copy in loads[:3]:
        copy.wait()
    values = frames_ref[...].astype(jnp.float32)
    mean_square = jnp.mean(values * values, axis=-1, keepdims=True)
    token = lax.broadcasted_iota(jnp.int32, (part, features), 0) + core * part
    gain = jnp.where(token < count, gain_a_ref[...].reshape(1, features), gain_v_ref[...].reshape(1, features))
    normed = (values * lax.rsqrt(mean_square + 1e-06) * gain).astype(jnp.bfloat16)
    for target in range(n_seq):
        stage[target] = normed[:, target * width : (target + 1) * width]
    for q in range(n_seq - 1, 0, -1):
        x1_copy(q, z).start()
    xbuf[x, z, mine, :] = stage[z]
    x2_copy(0, x).start()
    x3_copy(0, x, core, 0).start()
    for copy in own_weights:
        copy.wait()
    start_weights(0, early)

    rows = lax.broadcasted_iota(jnp.int32, (n_seq * tok, tok), 0)

    def place(column, q):
        about = meta[column, peers[q]]
        ints = about.astype(jnp.int32)
        block = jnp.bitwise_xor(ints[7:8, :], z)
        key = jnp.where(ints[8:9, :] == x, block * tok + ints[9:10, :], -1)
        piece = jnp.where(rows == key, 1.0, 0.0).astype(jnp.bfloat16)
        return piece, lax.dot_general(
            piece, about.astype(jnp.bfloat16), (((1,), (1,)), ((), ())), preferred_element_type=jnp.float32
        )

    def put(column, slot, q):
        piece, more = place(column, q)
        hot[:, (slot * n_seq + q) * tok : (slot * n_seq + q + 1) * tok] = piece
        return more

    facts = put(x, 0, 0)
    for q in range(1, n_seq):
        m1_copy(q, peers[q]).wait_recv()
        m2_copy(q, x).start()
    for q in range(1, n_seq):
        facts += put(x, 0, q)
    for q in range(1, n_seq):
        x1_copy(q, peers[q]).wait_recv()
        x2_copy(q, x).start()
        x3_copy(q, x, core, 0).start()
    start_weights(early, chunks)
    for q in range(n_seq):
        m2_copy(q, 1 - x).wait_recv()
        facts += put(1 - x, 1, q)
    pass_weights(0, early)

    def column_rows(column):
        return jnp.concatenate([xbuf[column, peers[q]] for q in range(n_seq)], axis=0)

    split = n_seq * tok
    for q in range(n_seq):
        x3_copy(q, x, 1 - core, 0).wait_recv()
        x2_copy(q, 1 - x).wait_recv()
        x3_copy(q, 1 - x, core, 1).start()
    sorted_rows = jnp.dot(hot[:, :split], column_rows(x), preferred_element_type=jnp.float32)
    for q in range(n_seq):
        x3_copy(q, 1 - x, 1 - core, 1).wait_recv()
    sorted_rows += jnp.dot(hot[:, split:], column_rows(1 - x), preferred_element_type=jnp.float32)
    is_audio = facts[:, 6:7] > 0.5
    lhs[:, :width] = jnp.where(is_audio, sorted_rows, 0.0).astype(jnp.bfloat16)
    lhs[:, width:] = jnp.where(is_audio, 0.0, sorted_rows).astype(jnp.bfloat16)

    def part_copy(out_slot, in_slot, c, peer):
        return pltpu.make_async_remote_copy(
            src_ref=outbox.at[out_slot, c],
            dst_ref=inbox.at[in_slot, c],
            send_sem=p_send.at[out_slot, c],
            recv_sem=p_recv.at[in_slot, c],
            device_id={"seq": peer},
            device_id_type=MESH,
        )

    def relay(c, carry):
        part_copy(2, 3, c, peers[1]).wait_recv()
        outbox[1, c] = (far[c] + inbox[3, c].astype(jnp.float32)).astype(jnp.bfloat16)
        part_copy(1, 1, c, peers[2]).start()
        return carry

    def near(c, carry):
        part_copy(0, 0, c, peers[1]).start()
        return carry

    def multiply(c, carry):
        @pl.when(c + early < chunks)
        def _():
            pass_weights(c + early, c + early + 1)

        weight_pass(c, 1 - group).wait_recv()
        cols = pl.ds(pl.multiple_of(c * chunk, chunk), chunk)
        product = jnp.dot(lhs[...], weights[:, cols], preferred_element_type=jnp.float32)
        outbox[0, c] = product[tok : 2 * tok, :].astype(jnp.bfloat16)
        outbox[2, c] = product[3 * tok :, :].astype(jnp.bfloat16)

        @pl.when(jnp.logical_not(inner))
        def _():
            part_copy(2, 3, c, peers[1]).start()
            outbox[1, c] = product[2 * tok : 3 * tok, :].astype(jnp.bfloat16)
            part_copy(1, 1, c, peers[2]).start()

        @pl.when(inner)
        def _():
            part_copy(2, 2, c, peers[3]).start()
            part_copy(0, 0, c, peers[1]).start()
            far[c] = product[2 * tok : 3 * tok, :]

        own[c] = product[:tok, :]
        return carry

    lax.fori_loop(0, chunks, multiply, 0)

    @pl.when(inner)
    def _():
        lax.fori_loop(0, chunks, relay, 0)

    @pl.when(jnp.logical_not(inner))
    def _():
        lax.fori_loop(0, chunks, near, 0)

    lanes = lax.broadcasted_iota(jnp.int32, (tok, HEAD), 1)
    pair = jnp.where(lanes < HEAD // 2, lanes, lanes - HEAD // 2)
    at = [facts[:tok, i : i + 1] * 64.0 + facts[:tok, i + 3 : i + 4] for i in range(3)]
    chosen = jnp.where(pair < HEAD // 8, at[0], jnp.where(pair < HEAD * 5 // 16, at[1], at[2]))
    angles = chosen * jnp.exp(pair.astype(jnp.float32) * (-2.0 / HEAD * math.log(1000000.0)))
    turn[0] = jnp.cos(angles)
    sinus = jnp.sin(angles)
    turn[1] = jnp.where(lanes < HEAD // 2, -sinus, sinus)

    def finish(c, carry):
        part_copy(0, 0, c, peers[1]).wait_recv()
        part_copy(1, 1, c, peers[2]).wait_recv()

        @pl.when(inner)
        def _():
            part_copy(2, 2, c, peers[3]).wait_recv()
            own[c] = own[c] + inbox[2, c].astype(jnp.float32)

        total = own[c] + inbox[0, c].astype(jnp.float32) + inbox[1, c].astype(jnp.float32)
        for h in range(chunk // HEAD):
            head = total[:, h * HEAD : (h + 1) * HEAD]
            turned = head * turn[0] + pltpu.roll(head, HEAD // 2, 1) * turn[1]
            cols = pl.ds(pl.multiple_of(c * chunk + h * HEAD, HEAD), HEAD)
            out_ref[:, cols] = turned.astype(out_ref.dtype)
        return carry

    lax.fori_loop(0, chunks, finish, 0)

    for q in range(n_seq):
        if q:
            x1_copy(q, z).wait_send()
            m1_copy(q, z).wait_send()
        x2_copy(q, x).wait_send()
        m2_copy(q, x).wait_send()
        x3_copy(q, x, core, 0).wait_send()
        x3_copy(q, 1 - x, core, 1).wait_send()

    def drain(c, carry):
        weight_copy(c, x).wait_send()
        weight_pass(c, group).wait_send()
        for slot in range(3):
            part_copy(slot, slot, c, peers[1]).wait_send()
        return carry

    lax.fori_loop(0, chunks, drain, 0)


def exchanged_plan(
    frames, audio_count, pos_ids, gain_audio, gain_video, audio_proj, video_proj, dest_device, dest_slot
):
    n_seq = lax.axis_size("seq")
    tok, features = frames.shape
    deep, columns = audio_proj.shape
    width = features // n_seq
    chunk = next(k for k in (2 * HEAD, HEAD) if columns % k == 0)
    chunks = columns // chunk
    early = min(2, chunks)
    vmem = pl.BlockSpec(memory_space=pltpu.VMEM)
    anywhere = pl.BlockSpec(memory_space=pl.ANY)
    dma = pltpu.SemaphoreType.DMA
    bf16, f32, i32 = jnp.bfloat16, jnp.float32, jnp.int32
    return pl.pallas_call(
        functools.partial(kernel, chunk, early),
        out_shape=jax.ShapeDtypeStruct((tok, columns), bf16),
        in_specs=[anywhere] * 9,
        out_specs=vmem,
        scratch_shapes=[
            pltpu.SMEM((1,), i32),
            pltpu.VMEM((tok // 2, features), bf16),
            pltpu.VMEM((3, tok), i32),
            pltpu.VMEM((1, tok), i32),
            pltpu.VMEM((1, tok), i32),
            pltpu.VMEM((features,), f32),
            pltpu.VMEM((features,), f32),
            pltpu.VMEM((2, n_seq, tok, width), bf16),
            pltpu.VMEM((n_seq, tok // 2, width), bf16),
            pltpu.VMEM((2, n_seq, META, tok), f32),
            pltpu.VMEM((n_seq * tok, 2 * n_seq * tok), bf16),
            pltpu.VMEM((n_seq * tok, 2 * width), bf16),
            pltpu.VMEM((2 * width, columns), bf16),
            pltpu.VMEM((3, chunks, tok, chunk), bf16),
            pltpu.VMEM((4, chunks, tok, chunk), bf16),
            pltpu.VMEM((chunks, tok, chunk), f32),
            pltpu.VMEM((chunks, tok, chunk), f32),
            pltpu.VMEM((2, tok, HEAD), f32),
            dma((7,)),
        ]
        + [dma((n_seq,))] * 8
        + [dma((2, n_seq))] * 2
        + [dma((2, chunks))] * 2
        + [dma((2,)), dma((3, chunks)), dma((4, chunks))],
        compiler_params=pltpu.CompilerParams(
            collective_id=0, has_side_effects=True, vmem_limit_bytes=60 * 1024 * 1024
        ),
    )(
        audio_count,
        frames,
        pos_ids,
        dest_device[None, :],
        dest_slot[None, :],
        gain_audio,
        gain_video,
        audio_proj,
        video_proj,
    )


def solution(mesh):
    in_specs = (
        P(("grp", "seq", "mdl"), None),
        P(("grp", "seq", "mdl")),
        P(None, ("grp", "seq", "mdl")),
        P(),
        P(),
        P(("seq", "mdl"), "sub"),
        P(("seq", "mdl"), "sub"),
        P(("grp", "seq", "mdl")),
        P(("grp", "seq", "mdl")),
    )
    out_specs = P(("grp", "seq", "mdl"), "sub")
    paired = (mesh.shape["seq"], mesh.shape["mdl"], mesh.shape["sub"]) == (4, 2, 2)
    plan = exchanged_plan if paired else gathered_plan
    return jax.shard_map(plan, mesh=mesh, in_specs=in_specs, out_specs=out_specs, check_vma=False)
```

```python
import functools
import math

import jax
import jax.numpy as jnp
from jax import lax
from jax.experimental import pallas as pl
from jax.experimental.pallas import tpu as pltpu
from jax.sharding import PartitionSpec as P

HEAD = 128
META = 16
MESH = pl.DeviceIdType.MESH


def normalize(frames, audio_mask, gain_audio, gain_video):
    values = frames.astype(jnp.float32)
    mean_square = jnp.mean(values * values, axis=-1, keepdims=True)
    row_gain = jnp.where(audio_mask[:, None], gain_audio[None, :], gain_video[None, :])
    return (values * lax.rsqrt(mean_square + 1e-06) * row_gain).astype(jnp.bfloat16)


def inverse_frequencies():
    exponent = -2.0 * jnp.arange(HEAD // 2).astype(jnp.float32) / HEAD
    return jnp.power(jnp.float32(1000000.0), exponent)


def rotate(values, positions):
    tok_rows = values.shape[0]
    half_size = HEAD // 2
    pair_index = jnp.arange(half_size, dtype=jnp.int32)[None, :]
    chosen = jnp.where(
        pair_index < HEAD // 8,
        positions[0][:, None],
        jnp.where(pair_index < HEAD * 5 // 16, positions[1][:, None], positions[2][:, None]),
    )
    angles = chosen.astype(jnp.float32) * inverse_frequencies()[None, :]
    cosine = jnp.cos(angles)[:, None, :]
    sinus = jnp.sin(angles)[:, None, :]
    by_head = values.reshape(tok_rows, -1, HEAD)
    lower = by_head[:, :, :half_size]
    second = by_head[:, :, half_size:]
    turned = jnp.concatenate(
        [lower * cosine - second * sinus, second * cosine + lower * sinus], axis=-1
    )
    return turned.reshape(tok_rows, -1)


def embed_rows(normed, audio_mask, positions, audio_proj, video_proj):
    from_audio = jnp.dot(
        normed,
        lax.all_gather(audio_proj, ("seq", "mdl"), axis=0, tiled=True),
        preferred_element_type=jnp.float32,
    )
    from_video = jnp.dot(
        normed,
        lax.all_gather(video_proj, ("seq", "mdl"), axis=0, tiled=True),
        preferred_element_type=jnp.float32,
    )
    selected = jnp.where(audio_mask[:, None], from_audio, from_video)
    return rotate(selected, positions).astype(jnp.bfloat16)


def gathered_plan(
    frames, audio_count, pos_ids, gain_audio, gain_video, audio_proj, video_proj, dest_device, dest_slot
):
    tok_rows = frames.shape[0]
    audio_mask = jnp.arange(tok_rows, dtype=jnp.int32) < audio_count[0]
    peer_count = lax.axis_size(("seq", "mdl"))
    capacity = 2 * tok_rows // peer_count
    onehot = (dest_device[:, None] == jnp.arange(peer_count, dtype=jnp.int32)[None, :]).astype(
        jnp.int32
    )
    arrival = jnp.sum(jnp.cumsum(onehot, axis=0) * onehot, axis=1) - 1
    bucket = dest_device * capacity + arrival
    normed = normalize(frames, audio_mask, gain_audio, gain_video)
    features = normed.shape[1]
    described = jnp.concatenate(
        [pos_ids.T, audio_mask.astype(jnp.int32)[:, None], dest_slot[:, None]], axis=1
    )
    outbox = jnp.zeros((peer_count * capacity, features), jnp.bfloat16).at[bucket].set(normed)
    blank_tags = jnp.concatenate(
        [
            jnp.zeros((peer_count * capacity, 4), jnp.int32),
            jnp.full((peer_count * capacity, 1), tok_rows, jnp.int32),
        ],
        axis=1,
    )
    tag_rows = blank_tags.at[bucket].set(described)
    received = lax.all_to_all(outbox, ("seq", "mdl"), split_axis=0, concat_axis=0, tiled=True)
    got_tags = lax.all_to_all(tag_rows, ("seq", "mdl"), split_axis=0, concat_axis=0, tiled=True)
    arrived = got_tags[:, 4]
    placed = jnp.zeros((tok_rows, features), jnp.bfloat16).at[arrived].set(received, mode="drop")
    placed_tags = jnp.zeros((tok_rows, 5), jnp.int32).at[arrived].set(got_tags, mode="drop")
    return embed_rows(placed, placed_tags[:, 3] > 0, placed_tags[:, :3].T, audio_proj, video_proj)


def kernel(
    chunk,
    early,
    count_hbm,
    frames_hbm,
    pos_hbm,
    dev_hbm,
    slot_hbm,
    gain_a_hbm,
    gain_v_hbm,
    audio_hbm,
    video_hbm,
    out_hbm,
    out_ref,
    count_ref,
    frames_ref,
    pos_ref,
    dev_ref,
    slot_ref,
    gain_a_ref,
    gain_v_ref,
    xbuf,
    stage,
    meta,
    hot,
    lhs,
    weights,
    outbox,
    inbox,
    own,
    far,
    turn,
    in_sem,
    x1_send,
    x1_recv,
    m1_send,
    m1_recv,
    x2_send,
    x2_recv,
    m2_send,
    m2_recv,
    x3_send,
    x3_recv,
    w_send,
    w_recv,
    w_own,
    p_send,
    p_recv,
    out_sem,
):
    n_seq = 4
    z = lax.axis_index("seq")
    x = lax.axis_index("mdl")
    core = lax.axis_index("sub")
    group = lax.axis_index("grp")
    features = frames_hbm.shape[1]
    tok = frames_hbm.shape[0]
    deep = audio_hbm.shape[0]
    width = features // n_seq
    chunks = audio_hbm.shape[1] // chunk
    part = tok // 2
    mine = pl.ds(pl.multiple_of(core * part, part), part)
    inner = jnp.logical_or(z == 1, z == 2)
    peers = (z, z + 1 - 2 * lax.rem(z, 2), lax.rem(z + 2, n_seq), n_seq - 1 - z)

    loads = [
        pltpu.make_async_copy(src, dst, in_sem.at[i])
        for i, (src, dst) in enumerate(
            (
                (frames_hbm.at[mine], frames_ref),
                (gain_a_hbm, gain_a_ref),
                (gain_v_hbm, gain_v_ref),
                (count_hbm, count_ref),
                (pos_hbm, pos_ref),
                (dev_hbm, dev_ref),
                (slot_hbm, slot_ref),
            )
        )
    ]
    for copy in loads:
        copy.start()

    barrier = pltpu.get_barrier_semaphore()
    for q in range(1, n_seq):
        pl.semaphore_signal(barrier, inc=1, device_id={"seq": peers[q]}, device_id_type=MESH)
    pl.semaphore_signal(barrier, inc=1, device_id={"mdl": 1 - x}, device_id_type=MESH)
    pl.semaphore_signal(barrier, inc=1, device_id={"sub": 1 - core}, device_id_type=MESH)
    pl.semaphore_signal(barrier, inc=1, device_id={"grp": 1 - group}, device_id_type=MESH)

    def weight_rows(kind, column):
        return pl.ds(pl.multiple_of(kind * width + column * deep, 16), deep)

    own_weights = [
        pltpu.make_async_copy(ref, weights.at[weight_rows(kind, x)], w_own.at[kind])
        for kind, ref in enumerate((audio_hbm, video_hbm))
    ]
    for copy in own_weights:
        copy.start()

    def weight_copy(c, column):
        at = weights.at[weight_rows(group, column), pl.ds(pl.multiple_of(c * chunk, chunk), chunk)]
        return pltpu.make_async_remote_copy(
            src_ref=weights.at[weight_rows(group, x), pl.ds(pl.multiple_of(c * chunk, chunk), chunk)],
            dst_ref=at,
            send_sem=w_send.at[0, c],
            recv_sem=w_recv.at[0, c],
            device_id={"mdl": 1 - x},
            device_id_type=MESH,
        )

    def weight_pass(c, kind):
        cols = pl.ds(pl.multiple_of(c * chunk, chunk), chunk)
        return pltpu.make_async_remote_copy(
            src_ref=weights.at[weight_rows(group, 1 - x), cols],
            dst_ref=weights.at[weight_rows(kind, 1 - x), cols],
            send_sem=w_send.at[1, c],
            recv_sem=w_recv.at[1, c],
            device_id={"grp": 1 - group},
            device_id_type=MESH,
        )

    def start_weights(first, last):
        def start(c, carry):
            weight_copy(c, x).start()
            return carry

        lax.fori_loop(first, last, start, 0)

    def pass_weights(first, last):
        def forward(c, carry):
            weight_copy(c, 1 - x).wait_recv()
            weight_pass(c, group).start()
            return carry

        lax.fori_loop(first, last, forward, 0)

    def x1_copy(q, source):
        return pltpu.make_async_remote_copy(
            src_ref=stage.at[peers[q]],
            dst_ref=xbuf.at[x, source, mine],
            send_sem=x1_send.at[q],
            recv_sem=x1_recv.at[q],
            device_id={"seq": peers[q]},
            device_id_type=MESH,
        )

    def m1_copy(q, source):
        return pltpu.make_async_remote_copy(
            src_ref=meta.at[x, z],
            dst_ref=meta.at[x, source],
            send_sem=m1_send.at[q],
            recv_sem=m1_recv.at[q],
            device_id={"seq": peers[q]},
            device_id_type=MESH,
        )

    def x2_copy(q, column):
        return pltpu.make_async_remote_copy(
            src_ref=xbuf.at[x, peers[q], mine],
            dst_ref=xbuf.at[column, peers[q], mine],
            send_sem=x2_send.at[q],
            recv_sem=x2_recv.at[q],
            device_id={"mdl": 1 - x},
            device_id_type=MESH,
        )

    def m2_copy(q, column):
        return pltpu.make_async_remote_copy(
            src_ref=meta.at[x, peers[q]],
            dst_ref=meta.at[column, peers[q]],
            send_sem=m2_send.at[q],
            recv_sem=m2_recv.at[q],
            device_id={"mdl": 1 - x},
            device_id_type=MESH,
        )

    def x3_copy(q, column, half, slot):
        rows = pl.ds(pl.multiple_of(half * part, part), part)
        return pltpu.make_async_remote_copy(
            src_ref=xbuf.at[column, peers[q], mine],
            dst_ref=xbuf.at[column, peers[q], rows],
            send_sem=x3_send.at[slot, q],
            recv_sem=x3_recv.at[slot, q],
            device_id={"sub": 1 - core},
            device_id_type=MESH,
        )

    for copy in loads[3:]:
        copy.wait()
    count = count_ref[0]
    lane = lax.broadcasted_iota(jnp.int32, (META, tok), 1)
    row = lax.broadcasted_iota(jnp.int32, (META, tok), 0)
    device = dev_ref[...]
    target_seq = device // 2
    lines = [pos_ref[i : i + 1, :] >> 6 for i in range(3)]
    lines += [pos_ref[i : i + 1, :] & 63 for i in range(3)]
    lines += [jnp.where(lane[0:1, :] < count, 1, 0)]
    lines += [target_seq, device - target_seq * 2, slot_ref[...]]
    table = jnp.zeros((META, tok), jnp.int32)
    for i, line in enumerate(lines):
        table = jnp.where(row == i, line, table)
    meta[x, z] = table.astype(jnp.float32)

    pl.semaphore_wait(barrier, n_seq + 2)
    for q in range(1, n_seq):
        m1_copy(q, z).start()
    m2_copy(0, x).start()

    for copy in loads[:3]:
        copy.wait()
    values = frames_ref[...].astype(jnp.float32)
    mean_square = jnp.mean(values * values, axis=-1, keepdims=True)
    token = lax.broadcasted_iota(jnp.int32, (part, features), 0) + core * part
    gain = jnp.where(token < count, gain_a_ref[...].reshape(1, features), gain_v_ref[...].reshape(1, features))
    normed = (values * lax.rsqrt(mean_square + 1e-06) * gain).astype(jnp.bfloat16)
    for target in range(n_seq):
        stage[target] = normed[:, target * width : (target + 1) * width]
    for q in range(1, n_seq):
        x1_copy(q, z).start()
    xbuf[x, z, mine, :] = stage[z]
    x2_copy(0, x).start()
    x3_copy(0, x, core, 0).start()
    for copy in own_weights:
        copy.wait()
    start_weights(0, early)

    rows = lax.broadcasted_iota(jnp.int32, (n_seq * tok, tok), 0)

    def place(column, q):
        about = meta[column, peers[q]]
        ints = about.astype(jnp.int32)
        block = jnp.bitwise_xor(ints[7:8, :], z)
        key = jnp.where(ints[8:9, :] == x, block * tok + ints[9:10, :], -1)
        piece = jnp.where(rows == key, 1.0, 0.0).astype(jnp.bfloat16)
        return piece, lax.dot_general(
            piece, about.astype(jnp.bfloat16), (((1,), (1,)), ((), ())), preferred_element_type=jnp.float32
        )

    def put(column, slot, q):
        piece, more = place(column, q)
        hot[:, (slot * n_seq + q) * tok : (slot * n_seq + q + 1) * tok] = piece
        return more

    facts = put(x, 0, 0)
    for q in range(1, n_seq):
        m1_copy(q, peers[q]).wait_recv()
        m2_copy(q, x).start()
    for q in range(1, n_seq):
        facts += put(x, 0, q)
    for q in range(1, n_seq):
        x1_copy(q, peers[q]).wait_recv()
        x2_copy(q, x).start()
        x3_copy(q, x, core, 0).start()
    start_weights(early, chunks)
    for q in range(n_seq):
        m2_copy(q, 1 - x).wait_recv()
        facts += put(1 - x, 1, q)
    pass_weights(0, early)

    def column_rows(column):
        return jnp.concatenate([xbuf[column, peers[q]] for q in range(n_seq)], axis=0)

    split = n_seq * tok
    for q in range(n_seq):
        x3_copy(q, x, 1 - core, 0).wait_recv()
        x2_copy(q, 1 - x).wait_recv()
        x3_copy(q, 1 - x, core, 1).start()
    sorted_rows = jnp.dot(hot[:, :split], column_rows(x), preferred_element_type=jnp.float32)
    for q in range(n_seq):
        x3_copy(q, 1 - x, 1 - core, 1).wait_recv()
    sorted_rows += jnp.dot(hot[:, split:], column_rows(1 - x), preferred_element_type=jnp.float32)
    is_audio = facts[:, 6:7] > 0.5
    lhs[:, :width] = jnp.where(is_audio, sorted_rows, 0.0).astype(jnp.bfloat16)
    lhs[:, width:] = jnp.where(is_audio, 0.0, sorted_rows).astype(jnp.bfloat16)

    def part_copy(out_slot, in_slot, c, peer):
        return pltpu.make_async_remote_copy(
            src_ref=outbox.at[out_slot, c],
            dst_ref=inbox.at[in_slot, c],
            send_sem=p_send.at[out_slot, c],
            recv_sem=p_recv.at[in_slot, c],
            device_id={"seq": peer},
            device_id_type=MESH,
        )

    def relay(c, carry):
        part_copy(2, 3, c, peers[1]).wait_recv()
        outbox[1, c] = (far[c] + inbox[3, c].astype(jnp.float32)).astype(jnp.bfloat16)
        part_copy(1, 1, c, peers[2]).start()
        return carry

    def near(c, carry):
        part_copy(0, 0, c, peers[1]).start()
        return carry

    def multiply(c, carry):
        @pl.when(c + early < chunks)
        def _():
            pass_weights(c + early, c + early + 1)

        weight_pass(c, 1 - group).wait_recv()
        cols = pl.ds(pl.multiple_of(c * chunk, chunk), chunk)
        product = jnp.dot(lhs[...], weights[:, cols], preferred_element_type=jnp.float32)
        outbox[0, c] = product[tok : 2 * tok, :].astype(jnp.bfloat16)
        outbox[2, c] = product[3 * tok :, :].astype(jnp.bfloat16)

        @pl.when(jnp.logical_not(inner))
        def _():
            part_copy(2, 3, c, peers[1]).start()
            outbox[1, c] = product[2 * tok : 3 * tok, :].astype(jnp.bfloat16)
            part_copy(1, 1, c, peers[2]).start()

        @pl.when(inner)
        def _():
            part_copy(2, 2, c, peers[3]).start()
            part_copy(0, 0, c, peers[1]).start()
            far[c] = product[2 * tok : 3 * tok, :]

        own[c] = product[:tok, :]
        return carry

    lax.fori_loop(0, chunks, multiply, 0)

    @pl.when(inner)
    def _():
        lax.fori_loop(0, chunks, relay, 0)

    @pl.when(jnp.logical_not(inner))
    def _():
        lax.fori_loop(0, chunks, near, 0)

    lanes = lax.broadcasted_iota(jnp.int32, (tok, HEAD), 1)
    pair = jnp.where(lanes < HEAD // 2, lanes, lanes - HEAD // 2)
    at = [facts[:tok, i : i + 1] * 64.0 + facts[:tok, i + 3 : i + 4] for i in range(3)]
    chosen = jnp.where(pair < HEAD // 8, at[0], jnp.where(pair < HEAD * 5 // 16, at[1], at[2]))
    angles = chosen * jnp.exp(pair.astype(jnp.float32) * (-2.0 / HEAD * math.log(1000000.0)))
    turn[0] = jnp.cos(angles)
    sinus = jnp.sin(angles)
    turn[1] = jnp.where(lanes < HEAD // 2, -sinus, sinus)

    def out_copy(c):
        cols = pl.ds(pl.multiple_of(c * chunk, chunk), chunk)
        return pltpu.make_async_copy(out_ref.at[:, cols], out_hbm.at[:, cols], out_sem.at[c])

    def finish(c, carry):
        part_copy(0, 0, c, peers[1]).wait_recv()
        part_copy(1, 1, c, peers[2]).wait_recv()

        @pl.when(inner)
        def _():
            part_copy(2, 2, c, peers[3]).wait_recv()
            own[c] = own[c] + inbox[2, c].astype(jnp.float32)

        total = own[c] + inbox[0, c].astype(jnp.float32) + inbox[1, c].astype(jnp.float32)
        for h in range(chunk // HEAD):
            head = total[:, h * HEAD : (h + 1) * HEAD]
            turned = head * turn[0] + pltpu.roll(head, HEAD // 2, 1) * turn[1]
            cols = pl.ds(pl.multiple_of(c * chunk + h * HEAD, HEAD), HEAD)
            out_ref[:, cols] = turned.astype(out_ref.dtype)
        out_copy(c).start()
        return carry

    lax.fori_loop(0, chunks, finish, 0)

    for q in range(n_seq):
        if q:
            x1_copy(q, z).wait_send()
            m1_copy(q, z).wait_send()
        x2_copy(q, x).wait_send()
        m2_copy(q, x).wait_send()
        x3_copy(q, x, core, 0).wait_send()
        x3_copy(q, 1 - x, core, 1).wait_send()

    def drain(c, carry):
        weight_copy(c, x).wait_send()
        weight_pass(c, group).wait_send()
        out_copy(c).wait()
        for slot in range(3):
            part_copy(slot, slot, c, peers[1]).wait_send()
        return carry

    lax.fori_loop(0, chunks, drain, 0)


def exchanged_plan(
    frames, audio_count, pos_ids, gain_audio, gain_video, audio_proj, video_proj, dest_device, dest_slot
):
    n_seq = lax.axis_size("seq")
    tok, features = frames.shape
    deep, columns = audio_proj.shape
    width = features // n_seq
    chunk = next(k for k in (2 * HEAD, HEAD) if columns % k == 0)
    chunks = columns // chunk
    early = min(2, chunks)
    anywhere = pl.BlockSpec(memory_space=pl.ANY)
    dma = pltpu.SemaphoreType.DMA
    bf16, f32, i32 = jnp.bfloat16, jnp.float32, jnp.int32
    return pl.pallas_call(
        functools.partial(kernel, chunk, early),
        out_shape=jax.ShapeDtypeStruct((tok, columns), bf16),
        in_specs=[anywhere] * 9,
        out_specs=anywhere,
        scratch_shapes=[
            pltpu.VMEM((tok, columns), bf16),
            pltpu.SMEM((1,), i32),
            pltpu.VMEM((tok // 2, features), bf16),
            pltpu.VMEM((3, tok), i32),
            pltpu.VMEM((1, tok), i32),
            pltpu.VMEM((1, tok), i32),
            pltpu.VMEM((features,), f32),
            pltpu.VMEM((features,), f32),
            pltpu.VMEM((2, n_seq, tok, width), bf16),
            pltpu.VMEM((n_seq, tok // 2, width), bf16),
            pltpu.VMEM((2, n_seq, META, tok), f32),
            pltpu.VMEM((n_seq * tok, 2 * n_seq * tok), bf16),
            pltpu.VMEM((n_seq * tok, 2 * width), bf16),
            pltpu.VMEM((2 * width, columns), bf16),
            pltpu.VMEM((3, chunks, tok, chunk), bf16),
            pltpu.VMEM((4, chunks, tok, chunk), bf16),
            pltpu.VMEM((chunks, tok, chunk), f32),
            pltpu.VMEM((chunks, tok, chunk), f32),
            pltpu.VMEM((2, tok, HEAD), f32),
            dma((7,)),
        ]
        + [dma((n_seq,))] * 8
        + [dma((2, n_seq))] * 2
        + [dma((2, chunks))] * 2
        + [dma((2,)), dma((3, chunks)), dma((4, chunks)), dma((chunks,))],
        compiler_params=pltpu.CompilerParams(
            collective_id=0, has_side_effects=True, vmem_limit_bytes=60 * 1024 * 1024
        ),
    )(
        audio_count,
        frames,
        pos_ids,
        dest_device[None, :],
        dest_slot[None, :],
        gain_audio,
        gain_video,
        audio_proj,
        video_proj,
    )


def solution(mesh):
    in_specs = (
        P(("grp", "seq", "mdl"), None),
        P(("grp", "seq", "mdl")),
        P(None, ("grp", "seq", "mdl")),
        P(),
        P(),
        P(("seq", "mdl"), "sub"),
        P(("seq", "mdl"), "sub"),
        P(("grp", "seq", "mdl")),
        P(("grp", "seq", "mdl")),
    )
    out_specs = P(("grp", "seq", "mdl"), "sub")
    paired = (mesh.shape["seq"], mesh.shape["mdl"], mesh.shape["sub"]) == (4, 2, 2)
    plan = exchanged_plan if paired else gathered_plan
    return jax.shard_map(plan, mesh=mesh, in_specs=in_specs, out_specs=out_specs, check_vma=False)
```
